1024 devices in a mesh: dp: 16 (over x_hi, z), shard: 64 (over x_lo, y, core).
Axes of the slice: x: 8 (x_hi: 2, x_lo: 4; x = x_hi * 4 + x_lo), y: 8, z: 8, core: 2. Of those that a mesh axis runs over, the one named last changes fastest.
Arguments:
- head_terms: bfloat16 [2048, 64, 256], P('dp', 'shard'), may hold values from -0.1875 to 0.1875
- inputs: bfloat16 [2048, 2, 4096], P('dp'), may hold values from -6 to 6
- owner_list: int32 [64, 256, 1], P('shard'), may hold values from 0 to 15; in each aligned block of 16 rows (0 to 15, 16 to 31, ..., all dimensions but the last counted through in order) at most 2 rows name the same one
- param_slots: bfloat16 [64, 512, 4096], P('shard', 'dp'), may hold values from -3 to 3
- row_state: float32 [64, 512], P('shard', 'dp'), may hold values from 0.25 to 4
- col_state: float32 [64, 4, 4096], P('shard'), may hold values from 0.25 to 4
Outputs:
- new_params: bfloat16 [64, 512, 4096], P('shard', 'dp')
- new_rows: float32 [64, 512], P('shard', 'dp')
- new_cols: float32 [64, 4, 4096], P('shard')
The draws below stay inside these ranges and needn't reach their ends.
Inputs may be any that keep to these rules, and one draw needn't show every extreme that they name: `owner_list`: each head's 256 rows fall into 16 aligned home blocks of 16 rows; within one home block no owner index is named more than 2 times.
All inputs are finite; a program needn't handle non-finite values.
Results may differ from the reference program's by a relative error of at most 0.0012.
Values sent between devices are 32-bit elements; how exact they have to be, the bound alone decides.
A program may use at most 64 MiB of HBM per device.

```python
import math
import jax
import jax.numpy as jnp
import numpy as np
from jax import lax

D = 4096
DKV = 64
PROJ = 4
HEADS = 64
ROWS_H = 256
TOKENS = 2048
BLOCK = 16
PAIR_MOST = 2
SLOTS = 32
N_DP = 16


def with_spikes(drawn, own_key, source, target, blocks, factor):
    def block_of(position):
        return (jnp.arange(drawn.shape[position]) // (drawn.shape[position] // blocks)).reshape((-1,) + (1,) * (drawn.ndim - 1 - position))

    one_side = jax.random.permutation(own_key, blocks)[block_of(target)]
    second = (block_of(target) + blocks // 2) % blocks
    return jnp.where((block_of(source) == one_side) | (block_of(source) == second), factor * drawn, drawn)


def block_scale(stream_key, dims, shards, smallest, high):
    loudness = 1.0
    for dim, parts in shards:
        draws = jax.random.uniform(jax.random.fold_in(jax.random.fold_in(stream_key, 6), dim), (parts,), jnp.float32, smallest / len(shards), high / len(shards))
        loudness = loudness * jnp.repeat(jnp.exp(draws), dims[dim] // parts).reshape((-1,) + (1,) * (len(dims) - 1 - dim))
    return loudness


def shared_out(stream_key, own, number, rows, count, top, reach, lean):
    order = jax.random.permutation(stream_key, count)
    crowded, usual = portions_of(count, rows * top, reach, lean, True), portions_of(count, rows * top, reach, lean, False)
    places = jnp.arange(count)

    def named(sizes, turn):
        used = int((sizes > 0).sum())
        fixed = max(1, used // 4)
        moved = fixed + (places - fixed + turn * (used - fixed)) % max(1, count - fixed)
        return jnp.zeros((count,), jnp.int32).at[order[jnp.where(places < fixed, places, moved)]].set(jnp.asarray(sizes, jnp.int32))

    sizes = jnp.where(number % 4 == 0, named(crowded, number // 4), named(usual, number - number // 4 - 1))
    mixed = jax.random.permutation(jax.random.fold_in(own, 3), count)
    giver, sink = mixed[0:count // 2 * 2:2], mixed[1:count // 2 * 2:2]
    margin = jnp.minimum(sizes[giver] - 1, reach - sizes[sink]) // 2
    margin = jnp.where((giver == order[0]) | (sink == order[0]) | (sizes[sink] == 0), 0, jnp.maximum(margin, 0))
    moved = jax.random.randint(jax.random.fold_in(own, 4), (count // 2,), 0, 1 << 20) % (margin + 1)
    sizes = sizes.at[giver].add(-moved).at[sink].add(moved)
    labels = jnp.searchsorted(jnp.cumsum(sizes), jnp.arange(rows * top), side="right").astype(jnp.int32)
    listing = labels.reshape(top, rows).T
    listing = listing[jax.random.permutation(jax.random.fold_in(own, 1), rows)]
    turn = jax.random.randint(jax.random.fold_in(own, 2), (rows, 1), 0, top)
    return jnp.take_along_axis(listing, (jnp.arange(top)[None, :] + turn) % top, axis=1)


def portions_of(amount, total, reach, lean, full):
    portions = [(1 << 20) // math.isqrt(grade ** lean) + 1 for grade in range(1, amount + 1)]
    largest = reach if full else min(reach, max(-(-total // amount), total * portions[0] // sum(portions)))
    least = 1 if total - largest >= amount - 1 else 0
    holding, surplus = [largest] + [least] * (amount - 1), total - largest - least * (amount - 1)
    while surplus > 0:
        free = [i for i in range(1, amount) if holding[i] < largest] or [i for i in range(1, amount) if holding[i] < reach]
        mass, budget = sum([portions[i] for i in free]), surplus
        for i in free:
            extra = min(reach - holding[i], max(1, budget * portions[i] // mass), surplus)
            holding[i] = holding[i] + extra
            surplus = surplus - extra
    return np.array(holding)


def centred(stream_key, shape, scale, bound, split=(), kind=jnp.bfloat16):
    factor_of = block_scale(stream_key, shape, split, -0.22, 0.18) if split else 1.0
    array = jax.random.normal(stream_key, shape, jnp.float32) * scale * factor_of
    return jnp.minimum(jnp.maximum(array, -bound), bound).astype(kind)


def noise_with(key, extent, scale, reach, cuts, heavy, kind=jnp.bfloat16):
    result = scale * jax.random.normal(key, extent, jnp.float32)
    if cuts:
        result = result * block_scale(key, extent, cuts, -0.22, 0.18)
    return jnp.clip(with_spikes(result, jax.random.fold_in(key, 3), *heavy), -reach, reach).astype(kind)


def setup_inputs(seed: int = 0) -> dict:
    arg_keys = jax.random.split(jax.random.key(seed), 7)
    head_terms = noise_with(arg_keys[0], (TOKENS, HEADS, ROWS_H), TOKENS ** -0.5, 0.1875, ((0, 16), (1, 64)), (0, 2, 16, 2.0))
    inputs = centred(arg_keys[1], (TOKENS, 2, D), 1.0, 6.0, ((0, 16),))
    owner_list_keys = jax.random.split(jax.random.fold_in(arg_keys[2], 1), HEADS * ROWS_H // BLOCK)
    owner_list_turns = jax.random.permutation(jax.random.fold_in(arg_keys[2], 3), HEADS * ROWS_H // BLOCK)
    owner_list = jax.vmap(lambda own, number: shared_out(jax.random.fold_in(arg_keys[2], 2), own, number, BLOCK, N_DP, 1, PAIR_MOST, 2))(owner_list_keys, owner_list_turns).reshape((HEADS, ROWS_H, 1))
    param_slots = centred(arg_keys[3], (HEADS, N_DP * SLOTS, D), 0.5, 3.0, ((0, 64), (1, 16)))
    row_state = jnp.clip(jnp.exp(math.log(4.0) - 2.7725887 * jax.random.uniform(arg_keys[4], (HEADS, N_DP * SLOTS), jnp.float32) ** block_scale(arg_keys[4], (HEADS, N_DP * SLOTS), ((0, 64), (1, 16)), -0.2, 0.2)), 0.25, 4.0)
    col_state = jnp.clip(jnp.exp(math.log(4.0) - 2.7725887 * jax.random.uniform(arg_keys[5], (HEADS, PROJ, D), jnp.float32) ** block_scale(arg_keys[5], (HEADS, PROJ, D), ((0, 64),), -0.2, 0.2)), 0.25, 4.0)
    return dict(head_terms=head_terms, inputs=inputs, owner_list=owner_list, param_slots=param_slots, row_state=row_state, col_state=col_state)


DECAY_RATE = 0.5
STEP_SIZE = 0.5
EPS_SQUARE = 1e-30

def slot_table(owner_col, owner_count, pair_most):
    row_count = owner_col.shape[0]
    block_rows = row_count // owner_count
    index_ids = jnp.arange(owner_count, dtype=jnp.int32)
    onehot = (owner_col[:, None] == index_ids[None, :]).astype(jnp.int32)
    blocked = onehot.reshape(owner_count, block_rows, owner_count)
    before = jnp.cumsum(blocked, axis=1) - blocked
    order_in = lax.optimization_barrier(jnp.sum(before * blocked, axis=2)).reshape(row_count)
    row_ids = jnp.arange(row_count, dtype=jnp.int32)
    block_of = row_ids // block_rows
    slot_ids = jnp.arange(pair_most, dtype=jnp.int32)
    match_owner = owner_col[None, None, None, :] == index_ids[:, None, None, None]
    match_block = block_of[None, None, None, :] == index_ids[None, :, None, None]
    match_slot = order_in[None, None, None, :] == slot_ids[None, None, :, None]
    hits = (match_owner & match_block & match_slot).astype(jnp.int32)
    live_mask = lax.optimization_barrier(jnp.sum(hits, axis=3)).reshape(owner_count, owner_count * pair_most)
    slot_row = lax.optimization_barrier(jnp.sum(hits * row_ids[None, None, None, :], axis=3)).reshape(owner_count, owner_count * pair_most)
    return (slot_row, live_mask)

def column_update(gradient, owner_col, params_col, rows_col, cols_col):
    slot_row, live_mask = slot_table(owner_col, N_DP, PAIR_MOST)
    flat_rows = slot_row.reshape(-1)
    live_f = live_mask.reshape(-1).astype(jnp.float32)
    grad_sq = gradient * gradient + EPS_SQUARE
    col_sum = lax.optimization_barrier(jnp.sum(grad_sq.reshape(PROJ, DKV, grad_sq.shape[1]), axis=1))
    new_col = DECAY_RATE * cols_col + (1.0 - DECAY_RATE) * col_sum / DKV
    row_sq = lax.optimization_barrier(jnp.mean(grad_sq, axis=1))
    row_val = DECAY_RATE * rows_col + (1.0 - DECAY_RATE) * jnp.take(row_sq, flat_rows)
    slot_pick = ((flat_rows // DKV)[:, None] == jnp.arange(PROJ, dtype=jnp.int32)[None, :]).astype(jnp.float32)
    row_mean = lax.optimization_barrier(jnp.sum(slot_pick * (row_val * live_f)[:, None], axis=0)) / DKV
    col_at = jnp.dot(slot_pick, new_col, precision=lax.Precision.HIGHEST)
    mean_at = lax.optimization_barrier(jnp.sum(slot_pick * row_mean[None, :], axis=1))
    second_moment = row_val[:, None] * col_at / mean_at[:, None]
    slot_grad = jnp.take(gradient, flat_rows, axis=0)
    update = slot_grad / jnp.sqrt(second_moment)
    new_param = ((params_col.astype(jnp.float32) - STEP_SIZE * update) * live_f[:, None]).astype(jnp.bfloat16)
    return (new_param, row_val * live_f, new_col)

def reference(head_terms, inputs, owner_list, param_slots, row_state, col_state):
    split_at = (PROJ - 1) * DKV

    def one_head(column_args):
        head_rows, owner_col, params_col, rows_col, cols_col = column_args
        first_part = jnp.dot(head_rows[:, :split_at].T, inputs[:, 0, :], preferred_element_type=jnp.float32)
        last_part = jnp.dot(head_rows[:, split_at:].T, inputs[:, 1, :], preferred_element_type=jnp.float32)
        gradient = jnp.concatenate([first_part, last_part], axis=0)
        return column_update(gradient, owner_col, params_col, rows_col, cols_col)
    new_params, new_rows, new_cols = lax.map(one_head, (jnp.transpose(head_terms, (1, 0, 2)), owner_list[:, :, 0], param_slots, row_state, col_state))
    return (new_params, new_rows, new_cols)
```

```python
import jax
import jax.numpy as jnp
from jax import lax
from jax.experimental import pallas as pl
from jax.experimental.pallas import tpu as pltpu
from jax.sharding import PartitionSpec as P

MESH = pl.DeviceIdType.MESH
EPS_SQUARE = 1e-30
F32 = jnp.float32
BF16 = jnp.bfloat16
NT = (((1,), (1,)), ((), ()))


def place():
    dp = lax.axis_index("dp")
    shard = lax.axis_index("shard")
    return dp, dp // 8, dp % 8, shard, shard // 16, (shard // 2) % 8, shard % 2


def kernel(hf, ip, own_row, own_col, rs_col, params, cols,
           out_p, out_r, out_c,
           hb, ib, hst, acc, gs, rb, sown, sb, pbuf, cbuf,
           ssh, rsh, ssi, rsi, ssy, rsy, ssc, rsc, sss, rss, ssg, rsg, loc):
    dp, a, z, shard, xl, y, c = place()
    other = 1 - a
    far_shard = (3 - xl) * 16 + y * 2 + c
    mate = xl * 16 + y * 2 + 1 - c
    fwd = lax.rem(y + 1 - 2 * c + 8, 8)
    back = lax.rem(y - 1 + 2 * c + 8, 8)
    fwd_shard = xl * 16 + fwd * 2 + c
    back_shard = xl * 16 + back * 2 + c
    right = (a * 8 + lax.rem(z + 1, 8), shard)
    left = (a * 8 + lax.rem(z + 7, 8), shard)

    def near(n):
        return a * 8 + lax.rem(z + n, 8)

    def far(n):
        return other * 8 + lax.rem(z + n, 8)

    peers = [near(n) for n in range(1, 8)] + [far(n) for n in range(8)]

    barrier = pltpu.get_barrier_semaphore()
    greeted = [(d, shard) for d in peers] + [(far(n), far_shard) for n in range(8)]
    greeted += [(dp, mate), (dp, fwd_shard), (dp, back_shard)]
    for who in greeted:
        pl.semaphore_signal(barrier, inc=1, device_id=who, device_id_type=MESH)

    local = [
        pltpu.make_async_copy(hf, hb.at[dp], loc.at[0]),
        pltpu.make_async_copy(ip.at[dp], ib.at[c, y, dp], loc.at[1]),
        pltpu.make_async_copy(params, pbuf, loc.at[2]),
        pltpu.make_async_copy(cols, cbuf, loc.at[3]),
    ]
    for cp in local:
        cp.start()

    pl.semaphore_wait(barrier, len(greeted))

    sent = []

    def send(src, dst, s_sem, r_sem, who):
        cp = pltpu.make_async_remote_copy(
            src_ref=src, dst_ref=dst, send_sem=s_sem, recv_sem=r_sem, device_id=who, device_id_type=MESH
        )
        cp.start()
        sent.append(cp)

    def arrived(ref, sem):
        pltpu.make_async_copy(ref, ref, sem).wait()

    count = [0]

    def send_h(d, who, src=None):
        send(hb.at[d] if src is None else src, hb.at[d], ssh.at[count[0]], rsh.at[d], who)
        count[0] += 1

    for i, n in enumerate((4, 3, 5, 2, 6, 1, 7, 0)):
        d = far(n)
        send(ip.at[d], ib.at[c, y, dp], ssi.at[i], rsi.at[dp], (d, far_shard))
    for i, n in enumerate((4, 3, 5, 2, 6, 1, 7)):
        d = near(n)
        send(ip.at[d], ib.at[c, y, dp], ssi.at[8 + i], rsi.at[dp], (d, shard))
    send_h(dp, (far(0), shard), hf)
    send_h(dp, right, hf)
    send_h(dp, left, hf)

    row_id = lax.broadcasted_iota(jnp.int32, (256, 256), 0)
    lane_id = lax.broadcasted_iota(jnp.int32, (256, 256), 1)
    owner = own_row[...]
    before = (own_col[...] == owner) & ((row_id >> 4) == (lane_id >> 4)) & (row_id < lane_id)
    rank = jnp.sum(before.astype(F32), axis=0, keepdims=True).astype(jnp.int32)
    rows = lax.broadcasted_iota(jnp.int32, (1, 256), 1)
    key = owner * 32 + (rows >> 4) * 2 + rank
    k0 = lax.broadcasted_iota(jnp.int32, (16, 24, 1), 0) * 32 + lax.broadcasted_iota(jnp.int32, (16, 24, 1), 1)
    k1 = lax.broadcasted_iota(jnp.int32, (16, 8, 1), 0) * 32 + 24 + lax.broadcasted_iota(jnp.int32, (16, 8, 1), 1)
    pick0 = (k0.reshape(384, 1) == key).astype(F32).astype(BF16)
    pick1 = (k1.reshape(128, 1) == key).astype(F32).astype(BF16)
    mine = lax.broadcasted_iota(jnp.int32, (32, 256), 0) + dp * 32
    live = jnp.sum((mine == key).astype(F32), axis=1, keepdims=True)
    slot8 = lax.broadcasted_iota(jnp.int32, (32, 128), 0) >> 3
    lane = lax.broadcasted_iota(jnp.int32, (32, 128), 1)
    sown[...] = jnp.sum(jnp.where(slot8 == (lane >> 5), live * rs_col[...], 0.0), axis=0, keepdims=True)
    for i, d in enumerate(peers):
        send(sown, sb.at[dp], sss.at[i], rss.at[dp], (d, shard))

    def got_h(d):
        arrived(hb.at[d], rsh.at[d])

    def send_y(yy, i, who):
        send(ib.at[c, yy], ib.at[c, yy], ssy.at[i], rsy.at[yy], (dp, who))

    def send_c(yy, i):
        send(ib.at[c, yy], ib.at[c, yy], ssc.at[i], rsc.at[yy], (dp, mate))

    def upstream(n):
        return lax.rem(y - n + 2 * n * c + 8, 8)

    def downstream(n):
        return lax.rem(y + n - 2 * n * c + 8, 8)

    def h_own(s):
        d = near(8 - s)
        got_h(d)
        if s < 4:
            send_h(d, right)
        if s < 4:
            d = near(s)
            got_h(d)
            if s < 3:
                send_h(d, left)

    def h_far(s):
        if s == 0:
            got_h(far(0))
            send_h(far(0), right)
            send_h(far(0), left)
            return
        if s < 4:
            d = far(8 - s)
            got_h(d)
            if s < 3:
                send_h(d, right)
        d = far(s)
        got_h(d)
        if s < 4:
            send_h(d, left)

    def i_ring(s):
        if s == 0:
            local[1].wait()
            for d in peers:
                arrived(ib.at[c, y, d], rsi.at[d])
            send_y(y, 0, fwd_shard)
            send_y(y, 1, back_shard)
            send_c(y, 0)
            return
        yy = upstream(s)
        arrived(ib.at[c, yy], rsy.at[yy])
        if s < 4:
            send_y(yy, 2 * s, fwd_shard)
        send_c(yy, 2 * s)
        if s < 4:
            yy = downstream(s)
            arrived(ib.at[c, yy], rsy.at[yy])
            if s < 3:
                send_y(yy, 2 * s + 1, back_shard)
            send_c(yy, 2 * s - 1)

    h_own(1)
    i_ring(0)
    h_far(0)
    h_own(2)
    h_far(1)
    i_ring(1)
    h_own(3)
    h_far(2)
    i_ring(2)
    h_own(4)
    h_far(3)
    i_ring(3)
    h_far(4)
    local[0].wait()

    for yy in range(8):
        h = hb[:, yy * 16:(yy + 1) * 16, :].reshape(256, 256).astype(BF16)
        hst[yy, 0:384, :] = lax.dot_general(pick0, h, NT, preferred_element_type=F32).astype(BF16)
        hst[yy, 384:512, :] = lax.dot_general(pick1, h, NT, preferred_element_type=F32).astype(BF16)

    i_ring(4)
    for n in range(8):
        yy = lax.rem(y + n, 8)
        arrived(ib.at[1 - c, yy], rsc.at[yy])

    acc[...] = jnp.zeros_like(acc)

    def tokens(yy, carry):
        w0 = ib[0, yy].reshape(256, 256).astype(BF16)
        w1 = ib[1, yy].reshape(256, 256).astype(BF16)
        acc[0:384, :] += jnp.dot(hst[yy, 0:384, :], w0, preferred_element_type=F32)
        acc[384:512, :] += jnp.dot(hst[yy, 384:512, :], w1, preferred_element_type=F32)
        return carry

    lax.fori_loop(0, 8, tokens, 0)

    for half in range(2):
        g0 = acc[0:384, half * 128:(half + 1) * 128].reshape(16, 24, 128)
        g1 = acc[384:512, half * 128:(half + 1) * 128].reshape(16, 8, 128)
        gs[:, half * 32:half * 32 + 24, :] = g0
        gs[:, half * 32 + 24:half * 32 + 32, :] = g1
        q0 = jnp.sum(jnp.sum((g0 * g0).reshape(16, 3, 8, 128), axis=0), axis=1)
        q1 = jnp.sum(jnp.sum(g1 * g1, axis=0), axis=0, keepdims=True)
        q = jnp.concatenate([q0, q1], axis=0)
        gs[:, 64 + half * 4:68 + half * 4, :] = jnp.broadcast_to(q[None], (16, 4, 128))

    for i, n in enumerate((4, 3, 5, 2, 6, 1, 7, 0)):
        d = far(n)
        send(gs.at[d], rb.at[dp], ssg.at[i], rsg.at[dp], (d, shard))
    for i, n in enumerate((4, 3, 5, 2, 6, 1, 7)):
        d = near(n)
        send(gs.at[d], rb.at[dp], ssg.at[8 + i], rsg.at[dp], (d, shard))
    keep = pltpu.make_async_copy(gs.at[dp], rb.at[dp], loc.at[4])
    keep.start()
    keep_s = pltpu.make_async_copy(sown, sb.at[dp], loc.at[5])
    keep_s.start()
    keep.wait()
    keep_s.wait()
    local[2].wait()
    local[3].wait()
    for d in peers:
        arrived(sb.at[d], rss.at[d])
    for d in peers:
        arrived(rb.at[d], rsg.at[d])

    sq = jnp.zeros((32, 128), F32)
    cs = jnp.zeros((4, 128), F32)
    for d in range(16):
        for half in range(2):
            g = rb[d, half * 32:half * 32 + 32, :]
            sq = sq + g * g
            cs = cs + rb[d, 64 + half * 4:68 + half * 4, :]
    row_val = 0.5 * rs_col[...] + 0.5 * (jnp.sum(sq, axis=1, keepdims=True) / 4096.0 + EPS_SQUARE)
    cs = cs + 64.0 * 32.0 * EPS_SQUARE
    all_cs = jnp.sum(jnp.broadcast_to(cs[:, None, :], (4, 8, 128)).reshape(32, 128), axis=1, keepdims=True)
    states = jnp.sum(sb[...], axis=0)
    all_st = jnp.sum(jnp.where(lane == slot8 * 32, states, 0.0), axis=1, keepdims=True)
    row_mean = (0.5 * all_st + 0.5 * (all_cs / 4096.0)) / 64.0
    by_row = 0.5 * lax.rsqrt(row_val / row_mean)
    out_r[...] = row_val * live
    for d in range(16):
        for half in range(2):
            at = d * 256 + half * 128
            q = rb[d, 64 + half * 4:68 + half * 4, :]
            new_col = 0.5 * cbuf[:, at:at + 128] + 0.5 * (q + 64.0 * EPS_SQUARE) / 64.0
            out_c[:, at:at + 128] = new_col
            by_col = jnp.broadcast_to(lax.rsqrt(new_col)[:, None, :], (4, 8, 128)).reshape(32, 128)
            g = rb[d, half * 32:half * 32 + 32, :]
            par = pbuf[:, at:at + 128].astype(F32)
            out_p[:, at:at + 128] = ((par - g * by_row * by_col) * live).astype(BF16)

    for cp in sent:
        cp.wait_send()


def on_device(head_terms, inputs, owner_list, param_slots, row_state, col_state):
    dp, a, z, shard, xl, y, c = place()
    hf = head_terms[:, 0, :].astype(F32)
    piece = lax.dynamic_slice(inputs, (16 * y, c, 0), (16, 1, 4096)).reshape(16, 16, 256)
    ip = jnp.transpose(piece, (1, 0, 2)).astype(F32)
    vm = pl.BlockSpec(memory_space=pltpu.VMEM)
    hbm = pl.BlockSpec(memory_space=pl.ANY)
    dma = pltpu.SemaphoreType.DMA
    new_params, new_rows, new_cols = pl.pallas_call(
        kernel,
        out_shape=(
            jax.ShapeDtypeStruct((32, 4096), BF16),
            jax.ShapeDtypeStruct((32, 1), F32),
            jax.ShapeDtypeStruct((4, 4096), F32),
        ),
        in_specs=[hbm, hbm, vm, vm, vm, hbm, hbm],
        out_specs=(vm, vm, vm),
        scratch_shapes=[
            pltpu.VMEM((16, 128, 256), F32),
            pltpu.VMEM((2, 8, 16, 16, 256), F32),
            pltpu.VMEM((8, 512, 256), BF16),
            pltpu.VMEM((512, 256), F32),
            pltpu.VMEM((16, 72, 128), F32),
            pltpu.VMEM((16, 72, 128), F32),
            pltpu.VMEM((1, 128), F32),
            pltpu.VMEM((16, 1, 128), F32),
            pltpu.VMEM((32, 4096), BF16),
            pltpu.VMEM((4, 4096), F32),
            dma((15,)), dma((16,)),
            dma((15,)), dma((16,)),
            dma((7,)), dma((8,)),
            dma((9,)), dma((8,)),
            dma((15,)), dma((16,)),
            dma((15,)), dma((16,)),
            dma((6,)),
        ],
        compiler_params=pltpu.CompilerParams(collective_id=0, has_side_effects=True, vmem_limit_bytes=40 << 20),
    )(
        hf,
        ip,
        owner_list.reshape(1, 256),
        owner_list.reshape(256, 1),
        row_state.reshape(32, 1),
        param_slots.reshape(32, 4096),
        col_state.reshape(4, 4096),
    )
    return (new_params[None], new_rows.reshape(1, 32), new_cols[None])


def solution(mesh):
    placed = (
        P("dp", "shard", None),
        P("dp", None, None),
        P("shard", None, None),
        P("shard", "dp", None),
        P("shard", "dp"),
        P("shard", None, None),
    )
    return jax.shard_map(
        on_device,
        mesh=mesh,
        in_specs=placed,
        out_specs=(P("shard", "dp", None), P("shard", "dp"), P("shard", None, None)),
        check_vma=False,
    )
```

```python
import jax
import jax.numpy as jnp
from jax import lax
from jax.experimental import pallas as pl
from jax.experimental.pallas import tpu as pltpu
from jax.sharding import PartitionSpec as P

MESH = pl.DeviceIdType.MESH
EPS_SQUARE = 1e-30
F32 = jnp.float32
BF16 = jnp.bfloat16
NT = (((1,), (1,)), ((), ()))


def place():
    dp = lax.axis_index("dp")
    shard = lax.axis_index("shard")
    return dp, dp // 8, dp % 8, shard, shard // 16, (shard // 2) % 8, shard % 2


def row_keys(owner):
    row_id = lax.broadcasted_iota(jnp.int32, (256, 256), 0)
    lane_id = lax.broadcasted_iota(jnp.int32, (256, 256), 1)
    same = (row_id == lane_id).astype(F32)
    own_col = jnp.sum(same * owner.astype(F32), axis=1, keepdims=True).astype(jnp.int32)
    before = (own_col == owner) & ((row_id >> 4) == (lane_id >> 4)) & (row_id < lane_id)
    rank = jnp.sum(before.astype(F32), axis=0, keepdims=True).astype(jnp.int32)
    rows = lax.broadcasted_iota(jnp.int32, (1, 256), 1)
    return owner * 32 + (rows >> 4) * 2 + rank


def own_slots(key, dp, states):
    mine = lax.broadcasted_iota(jnp.int32, (32, 256), 0) + dp * 32
    live = jnp.sum((mine == key).astype(F32), axis=1, keepdims=True)
    eye = lax.broadcasted_iota(jnp.int32, (32, 32), 0) == lax.broadcasted_iota(jnp.int32, (32, 32), 1)
    row_st = jnp.sum(jnp.where(eye, states, 0.0), axis=1, keepdims=True)
    return live, row_st, eye


def exchange(heads, inputs, owners, states, rb, sb,
             hraw, iraw, ipf, hb, ib, hst, acc, gs, sown,
             ssh, rsh, ssi, rsi, ssy, rsy, ssc, rsc, sss, rss, ssg, rsg, loc):
    dp, a, z, shard, xl, y, c = place()
    other = 1 - a
    far_shard = (3 - xl) * 16 + y * 2 + c
    mate = xl * 16 + y * 2 + 1 - c
    fwd = lax.rem(y + 1 - 2 * c + 8, 8)
    back = lax.rem(y - 1 + 2 * c + 8, 8)
    fwd_shard = xl * 16 + fwd * 2 + c
    back_shard = xl * 16 + back * 2 + c
    right = (a * 8 + lax.rem(z + 1, 8), shard)
    left = (a * 8 + lax.rem(z + 7, 8), shard)

    def near(n):
        return a * 8 + lax.rem(z + n, 8)

    def far(n):
        return other * 8 + lax.rem(z + n, 8)

    peers = [near(n) for n in range(1, 8)] + [far(n) for n in range(8)]

    barrier = pltpu.get_barrier_semaphore()
    greeted = [(d, shard) for d in peers] + [(far(n), far_shard) for n in range(8)]
    greeted += [(dp, mate), (dp, fwd_shard), (dp, back_shard)]
    for who in greeted:
        pl.semaphore_signal(barrier, inc=1, device_id=who, device_id_type=MESH)

    local = [
        pltpu.make_async_copy(inputs.at[pl.ds(16 * y, 16)], iraw, loc.at[0]),
        pltpu.make_async_copy(heads, hraw, loc.at[1]),
    ]
    for cp in local:
        cp.start()

    local[0].wait()
    which = lax.broadcasted_iota(jnp.int32, (16, 2, 256), 1) == c

    for d in range(16):
        pair = iraw[:, :, d * 256:(d + 1) * 256].astype(F32)
        ipf[d] = jnp.sum(jnp.where(which, pair, 0.0), axis=1)
    ib[c, y, dp] = ipf[dp]
    local[1].wait()
    hb[dp] = hraw[...].astype(F32)
    pl.semaphore_wait(barrier, len(greeted))

    sent = []

    def send(src, dst, s_sem, r_sem, who):
        cp = pltpu.make_async_remote_copy(
            src_ref=src, dst_ref=dst, send_sem=s_sem, recv_sem=r_sem, device_id=who, device_id_type=MESH
        )
        cp.start()
        sent.append(cp)

    def arrived(ref, sem):
        pltpu.make_async_copy(ref, ref, sem).wait()

    count = [0]

    def send_h(d, who):
        send(hb.at[d], hb.at[d], ssh.at[count[0]], rsh.at[d], who)
        count[0] += 1

    for i, n in enumerate((4, 3, 5, 2, 6, 1, 7, 0)):
        d = far(n)
        send(ipf.at[d], ib.at[c, y, dp], ssi.at[7 + i], rsi.at[dp], (d, far_shard))
    for i, n in enumerate((4, 3, 5, 2, 6, 1, 7)):
        d = near(n)
        send(ipf.at[d], ib.at[c, y, dp], ssi.at[i], rsi.at[dp], (d, shard))
    send_h(dp, (far(0), shard))
    send_h(dp, right)
    send_h(dp, left)

    key = row_keys(owners[...])
    k0 = lax.broadcasted_iota(jnp.int32, (16, 24, 1), 0) * 32 + lax.broadcasted_iota(jnp.int32, (16, 24, 1), 1)
    k1 = lax.broadcasted_iota(jnp.int32, (16, 8, 1), 0) * 32 + 24 + lax.broadcasted_iota(jnp.int32, (16, 8, 1), 1)
    pick0 = (k0.reshape(384, 1) == key).astype(F32).astype(BF16)
    pick1 = (k1.reshape(128, 1) == key).astype(F32).astype(BF16)
    live, row_st, _ = own_slots(key, dp, states[...])
    slot8 = lax.broadcasted_iota(jnp.int32, (32, 128), 0) >> 3
    lane = lax.broadcasted_iota(jnp.int32, (32, 128), 1)
    sown[...] = jnp.sum(jnp.where(slot8 == (lane >> 5), live * row_st, 0.0), axis=0, keepdims=True)
    for i, d in enumerate(peers):
        send(sown, sb.at[dp], sss.at[i], rss.at[dp], (d, shard))

    def got_h(d):
        arrived(hb.at[d], rsh.at[d])

    quads = (dp // 4, a * 2 + 1 - z // 4, other * 2 + z // 4, other * 2 + 1 - z // 4)

    def chunk(core, yy, g):
        return ib.at[core, yy, pl.ds(4 * quads[g], 4)]

    def send_y(yy, g, i, who):
        send(chunk(c, yy, g), chunk(c, yy, g), ssy.at[i, g], rsy.at[yy, g], (dp, who))

    def send_c(yy, g, i):
        send(chunk(c, yy, g), chunk(c, yy, g), ssc.at[i, g], rsc.at[yy, g], (dp, mate))

    def upstream(n):
        return lax.rem(y - n + 2 * n * c + 8, 8)

    def downstream(n):
        return lax.rem(y + n - 2 * n * c + 8, 8)

    def h_own(s):
        d = near(8 - s)
        got_h(d)
        if s < 4:
            send_h(d, right)
        if s < 4:
            d = near(s)
            got_h(d)
            if s < 3:
                send_h(d, left)

    def h_far(s):
        if s == 0:
            got_h(far(0))
            send_h(far(0), right)
            send_h(far(0), left)
            return
        if s < 4:
            d = far(8 - s)
            got_h(d)
            if s < 3:
                send_h(d, right)
        d = far(s)
        got_h(d)
        if s < 4:
            send_h(d, left)

    def i_ring(s, *groups):
        for g in groups:
            if s == 0:
                if g == 0:
                    for k in range(1, 4):
                        d = dp - z % 4 + lax.rem(z + k, 4)
                        arrived(ib.at[c, y, d], rsi.at[d])
                else:
                    for k in range(4):
                        d = 4 * quads[g] + k
                        arrived(ib.at[c, y, d], rsi.at[d])
                send_y(y, g, 0, fwd_shard)
                send_y(y, g, 1, back_shard)
                send_c(y, g, 0)
                continue
            yy = upstream(s)
            arrived(chunk(c, yy, g), rsy.at[yy, g])
            if s < 4:
                send_y(yy, g, 2 * s, fwd_shard)
            send_c(yy, g, 2 * s - 1)
            if s < 4:
                yy = downstream(s)
                arrived(chunk(c, yy, g), rsy.at[yy, g])
                if s < 3:
                    send_y(yy, g, 2 * s + 1, back_shard)
                send_c(yy, g, 2 * s)

    h_own(1)
    i_ring(0, 0, 1)
    h_far(0)
    h_own(2)
    i_ring(0, 2, 3)
    i_ring(1, 0, 1)
    h_far(1)
    i_ring(1, 2, 3)
    h_own(3)
    i_ring(2, 0, 1)
    h_far(2)
    i_ring(2, 2, 3)
    h_own(4)
    i_ring(3, 0, 1)
    h_far(3)
    i_ring(3, 2, 3)
    h_far(4)

    for yy in range(8):
        h = hb[:, yy * 16:(yy + 1) * 16, :].reshape(256, 256).astype(BF16)
        hst[yy, 0:384, :] = lax.dot_general(pick0, h, NT, preferred_element_type=F32).astype(BF16)
        hst[yy, 384:512, :] = lax.dot_general(pick1, h, NT, preferred_element_type=F32).astype(BF16)

    acc[...] = jnp.zeros_like(acc)

    def tokens(yy):
        for g in range(4):
            arrived(chunk(1 - c, yy, g), rsc.at[yy, g])
        w0 = ib[0, yy].reshape(256, 256).astype(BF16)
        w1 = ib[1, yy].reshape(256, 256).astype(BF16)
        acc[0:384, :] += jnp.dot(hst[yy, 0:384, :], w0, preferred_element_type=F32)
        acc[384:512, :] += jnp.dot(hst[yy, 384:512, :], w1, preferred_element_type=F32)

    tokens(y)
    for n in range(1, 4):
        tokens(lax.rem(y + n, 8))
        tokens(lax.rem(y + 8 - n, 8))
    i_ring(4, 0, 1, 2, 3)
    tokens(lax.rem(y + 4, 8))

    for half in range(2):
        g0 = acc[0:384, half * 128:(half + 1) * 128].reshape(16, 24, 128)
        g1 = acc[384:512, half * 128:(half + 1) * 128].reshape(16, 8, 128)
        gs[:, half * 32:half * 32 + 24, :] = g0
        gs[:, half * 32 + 24:half * 32 + 32, :] = g1
        q0 = jnp.sum(jnp.sum((g0 * g0).reshape(16, 3, 8, 128), axis=0), axis=1)
        q1 = jnp.sum(jnp.sum(g1 * g1, axis=0), axis=0, keepdims=True)
        q = jnp.concatenate([q0, q1], axis=0)
        gs[:, 64 + half * 4:68 + half * 4, :] = jnp.broadcast_to(q[None], (16, 4, 128))

    for i, n in enumerate((4, 3, 5, 2, 6, 1, 7, 0)):
        d = far(n)
        send(gs.at[d], rb.at[dp], ssg.at[i], rsg.at[dp], (d, shard))
    for i, n in enumerate((4, 3, 5, 2, 6, 1, 7)):
        d = near(n)
        send(gs.at[d], rb.at[dp], ssg.at[8 + i], rsg.at[dp], (d, shard))
    keep = [
        pltpu.make_async_copy(gs.at[dp], rb.at[dp], loc.at[2]),
        pltpu.make_async_copy(sown, sb.at[dp], loc.at[3]),
    ]
    for cp in keep:
        cp.start()
    for d in peers:
        arrived(sb.at[d], rss.at[d])
    for d in peers:
        arrived(rb.at[d], rsg.at[d])
    for cp in keep:
        cp.wait()
    for cp in sent:
        cp.wait_send()


def finish(rb, sb, owners, states, params, cols, out_p, out_r, out_c):
    live, row_st, eye = own_slots(row_keys(owners[...]), lax.axis_index("dp"), states[...])
    slot8 = lax.broadcasted_iota(jnp.int32, (32, 128), 0) >> 3
    lane = lax.broadcasted_iota(jnp.int32, (32, 128), 1)
    sq = jnp.zeros((32, 128), F32)
    cs = jnp.zeros((4, 128), F32)
    for d in range(16):
        for half in range(2):
            g = rb[d, half * 32:half * 32 + 32, :]
            sq = sq + g * g
            cs = cs + rb[d, 64 + half * 4:68 + half * 4, :]
    row_val = 0.5 * row_st + 0.5 * (jnp.sum(sq, axis=1, keepdims=True) / 4096.0 + EPS_SQUARE)
    cs = cs + 64.0 * 32.0 * EPS_SQUARE
    all_cs = jnp.sum(jnp.broadcast_to(cs[:, None, :], (4, 8, 128)).reshape(32, 128), axis=1, keepdims=True)
    all_sb = jnp.sum(sb[...], axis=0)
    all_st = jnp.sum(jnp.where(lane == slot8 * 32, all_sb, 0.0), axis=1, keepdims=True)
    row_mean = (0.5 * all_st + 0.5 * (all_cs / 4096.0)) / 64.0
    by_row = 0.5 * lax.rsqrt(row_val / row_mean)
    out_r[...] = jnp.sum(jnp.where(eye, row_val * live, 0.0), axis=0, keepdims=True)
    for d in range(16):
        for half in range(2):
            at = d * 256 + half * 128
            q = rb[d, 64 + half * 4:68 + half * 4, :]
            new_col = 0.5 * cols[:, at:at + 128] + 0.5 * (q + 64.0 * EPS_SQUARE) / 64.0
            out_c[:, at:at + 128] = new_col
            by_col = jnp.broadcast_to(lax.rsqrt(new_col)[:, None, :], (4, 8, 128)).reshape(32, 128)
            g = rb[d, half * 32:half * 32 + 32, :]
            par = params[:, at:at + 128].astype(F32)
            out_p[:, at:at + 128] = ((par - g * by_row * by_col) * live).astype(BF16)


def on_device(head_terms, inputs, owner_list, param_slots, row_state, col_state):
    vm = pl.BlockSpec(memory_space=pltpu.VMEM)
    hbm = pl.BlockSpec(memory_space=pl.ANY)
    dma = pltpu.SemaphoreType.DMA
    owners = owner_list.reshape(1, 256)
    rb, sb = pl.pallas_call(
        exchange,
        out_shape=(jax.ShapeDtypeStruct((16, 72, 128), F32), jax.ShapeDtypeStruct((16, 1, 128), F32)),
        in_specs=[hbm, hbm, vm, vm],
        out_specs=(hbm, hbm),
        scratch_shapes=[
            pltpu.VMEM((128, 256), BF16),
            pltpu.VMEM((16, 2, 4096), BF16),
            pltpu.VMEM((16, 16, 256), F32),
            pltpu.VMEM((16, 128, 256), F32),
            pltpu.VMEM((2, 8, 16, 16, 256), F32),
            pltpu.VMEM((8, 512, 256), BF16),
            pltpu.VMEM((512, 256), F32),
            pltpu.VMEM((16, 72, 128), F32),
            pltpu.VMEM((1, 128), F32),
            dma((15,)), dma((16,)),
            dma((15,)), dma((16,)),
            dma((7, 4)), dma((8, 4)),
            dma((8, 4)), dma((8, 4)),
            dma((15,)), dma((16,)),
            dma((15,)), dma((16,)),
            dma((4,)),
        ],
        compiler_params=pltpu.CompilerParams(collective_id=0, has_side_effects=True),
    )(head_terms.reshape(128, 256), inputs, owners, row_state)
    new_params, new_rows, new_cols = pl.pallas_call(
        finish,
        out_shape=(
            jax.ShapeDtypeStruct((32, 4096), BF16),
            jax.ShapeDtypeStruct((1, 32), F32),
            jax.ShapeDtypeStruct((4, 4096), F32),
        ),
        in_specs=[vm] * 6,
        out_specs=(vm, vm, vm),
    )(rb, sb, owners, row_state, param_slots.reshape(32, 4096), col_state.reshape(4, 4096))
    return (new_params[None], new_rows, new_cols[None])


def solution(mesh):
    placed = (
        P("dp", "shard", None),
        P("dp", None, None),
        P("shard", None, None),
        P("shard", "dp", None),
        P("shard", "dp"),
        P("shard", None, None),
    )
    return jax.shard_map(
        on_device,
        mesh=mesh,
        in_specs=placed,
        out_specs=(P("shard", "dp", None), P("shard", "dp"), P("shard", None, None)),
        check_vma=False,
    )
```

```python
import jax
import jax.numpy as jnp
from jax import lax
from jax.experimental import pallas as pl
from jax.experimental.pallas import tpu as pltpu
from jax.sharding import PartitionSpec as P

MESH = pl.DeviceIdType.MESH
EPS_SQUARE = 1e-30
F32 = jnp.float32
BF16 = jnp.bfloat16
NT = (((1,), (1,)), ((), ()))


def place():
    dp = lax.axis_index("dp")
    shard = lax.axis_index("shard")
    return dp, dp // 8, dp % 8, shard, shard // 16, (shard // 2) % 8, shard % 2


def row_keys(owner):
    row_id = lax.broadcasted_iota(jnp.int32, (256, 256), 0)
    lane_id = lax.broadcasted_iota(jnp.int32, (256, 256), 1)
    same = (row_id == lane_id).astype(F32)
    own_col = jnp.sum(same * owner.astype(F32), axis=1, keepdims=True).astype(jnp.int32)
    before = (own_col == owner) & ((row_id >> 4) == (lane_id >> 4)) & (row_id < lane_id)
    rank = jnp.sum(before.astype(F32), axis=0, keepdims=True).astype(jnp.int32)
    rows = lax.broadcasted_iota(jnp.int32, (1, 256), 1)
    return owner * 32 + (rows >> 4) * 2 + rank


def own_slots(key, dp, states):
    mine = lax.broadcasted_iota(jnp.int32, (32, 256), 0) + dp * 32
    live = jnp.sum((mine == key).astype(F32), axis=1, keepdims=True)
    eye = lax.broadcasted_iota(jnp.int32, (32, 32), 0) == lax.broadcasted_iota(jnp.int32, (32, 32), 1)
    row_st = jnp.sum(jnp.where(eye, states, 0.0), axis=1, keepdims=True)
    return live, row_st, eye


def exchange(heads, inputs, owners, states, rb, sb,
             hraw, iraw, ipf, hb, ib, hst, ibf, acc, gs, sown,
             ssh, rsh, ssi, rsi, ssy, rsy, ssc, rsc, sss, rss, ssg, rsg, loc):
    dp, a, z, shard, xl, y, c = place()
    other = 1 - a
    far_shard = (3 - xl) * 16 + y * 2 + c
    mate = xl * 16 + y * 2 + 1 - c
    fwd = lax.rem(y + 1 - 2 * c + 8, 8)
    back = lax.rem(y - 1 + 2 * c + 8, 8)
    fwd_shard = xl * 16 + fwd * 2 + c
    back_shard = xl * 16 + back * 2 + c
    right = (a * 8 + lax.rem(z + 1, 8), shard)
    left = (a * 8 + lax.rem(z + 7, 8), shard)

    def near(n):
        return a * 8 + lax.rem(z + n, 8)

    def far(n):
        return other * 8 + lax.rem(z + n, 8)

    peers = [near(n) for n in range(1, 8)] + [far(n) for n in range(8)]

    barrier = pltpu.get_barrier_semaphore()
    greeted = [(d, shard) for d in peers] + [(far(n), far_shard) for n in range(8)]
    greeted += [(dp, mate), (dp, fwd_shard), (dp, back_shard)]
    for who in greeted:
        pl.semaphore_signal(barrier, inc=1, device_id=who, device_id_type=MESH)

    local = [
        pltpu.make_async_copy(inputs.at[pl.ds(16 * y, 16)], iraw, loc.at[0]),
        pltpu.make_async_copy(heads, hraw, loc.at[1]),
    ]
    for cp in local:
        cp.start()

    local[1].wait()
    hb[dp] = hraw[...].astype(F32)
    local[0].wait()
    which = lax.broadcasted_iota(jnp.int32, (16, 2, 256), 1) == c

    def widen(d):
        at = pl.ds(pl.multiple_of(d * 256, 256), 256)
        ipf[d] = jnp.sum(jnp.where(which, iraw[:, :, at].astype(F32), 0.0), axis=1)

    pl.semaphore_wait(barrier, len(greeted))

    sent = []

    def send(src, dst, s_sem, r_sem, who):
        cp = pltpu.make_async_remote_copy(
            src_ref=src, dst_ref=dst, send_sem=s_sem, recv_sem=r_sem, device_id=who, device_id_type=MESH
        )
        cp.start()
        sent.append(cp)

    def arrived(ref, sem):
        pltpu.make_async_copy(ref, ref, sem).wait()

    count = [0]

    def piece(d, p):
        return hb.at[d, pl.ds(64 * p, 64)]

    def send_h(d, p, who):
        send(piece(d, p), piece(d, p), ssh.at[count[0]], rsh.at[d, p], who)
        count[0] += 1

    for p in range(2):
        send_h(dp, p, (far(0), shard))
    for i, n in enumerate((1, 7, 2, 6, 3, 5, 4)):
        d = near(n)
        widen(d)
        send(ipf.at[d], ib.at[c, y, dp], ssi.at[i], rsi.at[dp], (d, shard))
    for p in range(2):
        send_h(dp, p, right)
        send_h(dp, p, left)
    for i, n in enumerate((4, 3, 5, 2, 6, 1, 7, 0)):
        d = far(n)
        widen(d)
        send(ipf.at[d], ib.at[c, y, dp], ssi.at[7 + i], rsi.at[dp], (d, far_shard))

    widen(dp)
    ib[c, y, dp] = ipf[dp]

    key = row_keys(owners[...])
    k0 = lax.broadcasted_iota(jnp.int32, (16, 24, 1), 0) * 32 + lax.broadcasted_iota(jnp.int32, (16, 24, 1), 1)
    k1 = lax.broadcasted_iota(jnp.int32, (16, 8, 1), 0) * 32 + 24 + lax.broadcasted_iota(jnp.int32, (16, 8, 1), 1)
    pick0 = (k0.reshape(384, 1) == key).astype(F32).astype(BF16)
    pick1 = (k1.reshape(128, 1) == key).astype(F32).astype(BF16)
    live, row_st, _ = own_slots(key, dp, states[...])
    slot8 = lax.broadcasted_iota(jnp.int32, (32, 128), 0) >> 3
    lane = lax.broadcasted_iota(jnp.int32, (32, 128), 1)
    sown[...] = jnp.sum(jnp.where(slot8 == (lane >> 5), live * row_st, 0.0), axis=0, keepdims=True)
    for i, d in enumerate(peers):
        send(sown, sb.at[dp], sss.at[i], rss.at[dp], (d, shard))

    def got_h(d, p):
        arrived(piece(d, p), rsh.at[d, p])

    def pick_h(d):
        at = pl.ds(pl.multiple_of(d * 128, 128), 128)
        h = hb[d].astype(BF16)
        hst[0:384, at] = lax.dot_general(pick0, h, NT, preferred_element_type=F32).astype(BF16)
        hst[384:512, at] = lax.dot_general(pick1, h, NT, preferred_element_type=F32).astype(BF16)

    def narrow(core, yy, g):
        at = pl.ds(4 * quads[g], 4)
        ibf[core, at, yy] = ib[core, yy, at].astype(BF16)

    quads = (dp // 4, a * 2 + 1 - z // 4, other * 2 + z // 4, other * 2 + 1 - z // 4)

    def chunk(core, yy, g):
        return ib.at[core, yy, pl.ds(4 * quads[g], 4)]

    def send_y(yy, g, i, who):
        send(chunk(c, yy, g), chunk(c, yy, g), ssy.at[i, g], rsy.at[yy, g], (dp, who))

    def send_c(yy, g, i):
        send(chunk(c, yy, g), chunk(c, yy, g), ssc.at[i, g], rsc.at[yy, g], (dp, mate))

    def upstream(n):
        return lax.rem(y - n + 2 * n * c + 8, 8)

    def downstream(n):
        return lax.rem(y + n - 2 * n * c + 8, 8)

    def h_own(s):
        d, e = near(8 - s), near(s)
        for p in range(2):
            got_h(d, p)
            if s < 4:
                send_h(d, p, right)
                got_h(e, p)
                if s < 3:
                    send_h(e, p, left)
        pick_h(d)
        if s < 4:
            pick_h(e)

    def h_far(s):
        d, e = far(8 - s), far(s)
        for p in range(2):
            if 0 < s < 4:
                got_h(d, p)
                if s < 3:
                    send_h(d, p, right)
            got_h(e, p)
            if s == 0:
                send_h(e, p, right)
            if s < 4:
                send_h(e, p, left)
        if 0 < s < 4:
            pick_h(d)
        pick_h(e)

    def i_ring(s, *groups):
        for g in groups:
            if s == 0:
                for k in range(1 if g == 0 else 0, 4):
                    d = dp - z % 4 + lax.rem(z + k, 4) if g == 0 else 4 * quads[g] + k
                    arrived(ib.at[c, y, d], rsi.at[d])
                send_y(y, g, 0, fwd_shard)
                send_y(y, g, 1, back_shard)
                send_c(y, g, 0)
                narrow(c, y, g)
                continue
            up = upstream(s)
            arrived(chunk(c, up, g), rsy.at[up, g])
            if s < 4:
                send_y(up, g, 2 * s, fwd_shard)
            send_c(up, g, 2 * s - 1)
            if s < 4:
                down = downstream(s)
                arrived(chunk(c, down, g), rsy.at[down, g])
                if s < 3:
                    send_y(down, g, 2 * s + 1, back_shard)
                send_c(down, g, 2 * s)
                narrow(c, down, g)
            narrow(c, up, g)

    def tokens(g):
        for n in range(8):
            yy = lax.rem(y + n, 8)
            arrived(chunk(1 - c, yy, g), rsc.at[yy, g])
            narrow(1 - c, yy, g)
        at = pl.ds(pl.multiple_of(quads[g] * 512, 512), 512)
        w0 = ibf[0, pl.ds(4 * quads[g], 4)].reshape(512, 256)
        w1 = ibf[1, pl.ds(4 * quads[g], 4)].reshape(512, 256)
        g0 = jnp.dot(hst[0:384, at], w0, preferred_element_type=F32)
        g1 = jnp.dot(hst[384:512, at], w1, preferred_element_type=F32)
        if g == 0:
            acc[0:384, :] = g0
            acc[384:512, :] = g1
        else:
            acc[0:384, :] += g0
            acc[384:512, :] += g1

    pick_h(dp)
    h_own(1)
    i_ring(0, 0, 1)
    h_far(0)
    h_own(2)
    i_ring(0, 2, 3)
    i_ring(1, 0, 1)
    h_far(1)
    i_ring(1, 2, 3)
    h_own(3)
    i_ring(2, 0, 1)
    h_far(2)
    i_ring(2, 2, 3)
    h_own(4)
    i_ring(3, 0, 1)
    h_far(3)
    i_ring(3, 2, 3)
    i_ring(4, 0, 1)
    tokens(0)
    tokens(1)
    h_far(4)
    i_ring(4, 2, 3)
    tokens(2)
    tokens(3)

    for half in range(2):
        g0 = acc[0:384, half * 128:(half + 1) * 128].reshape(16, 24, 128)
        g1 = acc[384:512, half * 128:(half + 1) * 128].reshape(16, 8, 128)
        gs[:, half * 32:half * 32 + 24, :] = g0
        gs[:, half * 32 + 24:half * 32 + 32, :] = g1
        q0 = jnp.sum(jnp.sum((g0 * g0).reshape(16, 3, 8, 128), axis=0), axis=1)
        q1 = jnp.sum(jnp.sum(g1 * g1, axis=0), axis=0, keepdims=True)
        q = jnp.concatenate([q0, q1], axis=0)
        gs[:, 64 + half * 4:68 + half * 4, :] = jnp.broadcast_to(q[None], (16, 4, 128))

    for i, n in enumerate((4, 3, 5, 2, 6, 1, 7, 0)):
        d = far(n)
        send(gs.at[d], rb.at[dp], ssg.at[i], rsg.at[dp], (d, shard))
    for i, n in enumerate((4, 3, 5, 2, 6, 1, 7)):
        d = near(n)
        send(gs.at[d], rb.at[dp], ssg.at[8 + i], rsg.at[dp], (d, shard))
    keep = [
        pltpu.make_async_copy(gs.at[dp], rb.at[dp], loc.at[2]),
        pltpu.make_async_copy(sown, sb.at[dp], loc.at[3]),
    ]
    for cp in keep:
        cp.start()
    for d in peers:
        arrived(sb.at[d], rss.at[d])
    for d in peers:
        arrived(rb.at[d], rsg.at[d])
    for cp in keep:
        cp.wait()
    for cp in sent:
        cp.wait_send()


def finish(rb, sb, owners, states, params, cols, out_p, out_r, out_c):
    live, row_st, eye = own_slots(row_keys(owners[...]), lax.axis_index("dp"), states[...])
    slot8 = lax.broadcasted_iota(jnp.int32, (32, 128), 0) >> 3
    lane = lax.broadcasted_iota(jnp.int32, (32, 128), 1)
    sq = jnp.zeros((32, 128), F32)
    cs = jnp.zeros((4, 128), F32)
    for d in range(16):
        for half in range(2):
            g = rb[d, half * 32:half * 32 + 32, :]
            sq = sq + g * g
            cs = cs + rb[d, 64 + half * 4:68 + half * 4, :]
    row_val = 0.5 * row_st + 0.5 * (jnp.sum(sq, axis=1, keepdims=True) / 4096.0 + EPS_SQUARE)
    cs = cs + 64.0 * 32.0 * EPS_SQUARE
    all_cs = jnp.sum(jnp.broadcast_to(cs[:, None, :], (4, 8, 128)).reshape(32, 128), axis=1, keepdims=True)
    all_sb = jnp.sum(sb[...], axis=0)
    all_st = jnp.sum(jnp.where(lane == slot8 * 32, all_sb, 0.0), axis=1, keepdims=True)
    row_mean = (0.5 * all_st + 0.5 * (all_cs / 4096.0)) / 64.0
    by_row = 0.5 * lax.rsqrt(row_val / row_mean)
    out_r[...] = jnp.sum(jnp.where(eye, row_val * live, 0.0), axis=0, keepdims=True)
    for d in range(16):
        for half in range(2):
            at = d * 256 + half * 128
            q = rb[d, 64 + half * 4:68 + half * 4, :]
            new_col = 0.5 * cols[:, at:at + 128] + 0.5 * (q + 64.0 * EPS_SQUARE) / 64.0
            out_c[:, at:at + 128] = new_col
            by_col = jnp.broadcast_to(lax.rsqrt(new_col)[:, None, :], (4, 8, 128)).reshape(32, 128)
            g = rb[d, half * 32:half * 32 + 32, :]
            par = params[:, at:at + 128].astype(F32)
            out_p[:, at:at + 128] = ((par - g * by_row * by_col) * live).astype(BF16)


def on_device(head_terms, inputs, owner_list, param_slots, row_state, col_state):
    vm = pl.BlockSpec(memory_space=pltpu.VMEM)
    hbm = pl.BlockSpec(memory_space=pl.ANY)
    dma = pltpu.SemaphoreType.DMA
    owners = owner_list.reshape(1, 256)
    rb, sb = pl.pallas_call(
        exchange,
        out_shape=(jax.ShapeDtypeStruct((16, 72, 128), F32), jax.ShapeDtypeStruct((16, 1, 128), F32)),
        in_specs=[hbm, hbm, vm, vm],
        out_specs=(hbm, hbm),
        scratch_shapes=[
            pltpu.VMEM((128, 256), BF16),
            pltpu.VMEM((16, 2, 4096), BF16),
            pltpu.VMEM((16, 16, 256), F32),
            pltpu.VMEM((16, 128, 256), F32),
            pltpu.VMEM((2, 8, 16, 16, 256), F32),
            pltpu.VMEM((512, 2048), BF16),
            pltpu.VMEM((2, 16, 8, 16, 256), BF16),
            pltpu.VMEM((512, 256), F32),
            pltpu.VMEM((16, 72, 128), F32),
            pltpu.VMEM((1, 128), F32),
            dma((30,)), dma((16, 2)),
            dma((15,)), dma((16,)),
            dma((7, 4)), dma((8, 4)),
            dma((8, 4)), dma((8, 4)),
            dma((15,)), dma((16,)),
            dma((15,)), dma((16,)),
            dma((4,)),
        ],
        compiler_params=pltpu.CompilerParams(collective_id=0, has_side_effects=True),
    )(head_terms.reshape(128, 256), inputs, owners, row_state)
    new_params, new_rows, new_cols = pl.pallas_call(
        finish,
        out_shape=(
            jax.ShapeDtypeStruct((32, 4096), BF16),
            jax.ShapeDtypeStruct((1, 32), F32),
            jax.ShapeDtypeStruct((4, 4096), F32),
        ),
        in_specs=[vm] * 6,
        out_specs=(vm, vm, vm),
    )(rb, sb, owners, row_state, param_slots.reshape(32, 4096), col_state.reshape(4, 4096))
    return (new_params[None], new_rows, new_cols[None])


def solution(mesh):
    placed = (
        P("dp", "shard", None),
        P("dp", None, None),
        P("shard", None, None),
        P("shard", "dp", None),
        P("shard", "dp"),
        P("shard", None, None),
    )
    return jax.shard_map(
        on_device,
        mesh=mesh,
        in_specs=placed,
        out_specs=(P("shard", "dp", None), P("shard", "dp"), P("shard", None, None)),
        check_vma=False,
    )
```

```python
import jax
import jax.numpy as jnp
from jax import lax
from jax.experimental import pallas as pl
from jax.experimental.pallas import tpu as pltpu
from jax.sharding import PartitionSpec as P

MESH = pl.DeviceIdType.MESH
EPS_SQUARE = 1e-30
F32 = jnp.float32
BF16 = jnp.bfloat16
NT = (((1,), (1,)), ((), ()))


def place():
    dp = lax.axis_index("dp")
    shard = lax.axis_index("shard")
    return dp, dp // 8, dp % 8, shard, shard // 16, (shard // 2) % 8, shard % 2


def row_keys(owner):
    row_id = lax.broadcasted_iota(jnp.int32, (256, 256), 0)
    lane_id = lax.broadcasted_iota(jnp.int32, (256, 256), 1)
    same = (row_id == lane_id).astype(F32)
    own_col = jnp.sum(same * owner.astype(F32), axis=1, keepdims=True).astype(jnp.int32)
    before = (own_col == owner) & ((row_id >> 4) == (lane_id >> 4)) & (row_id < lane_id)
    rank = jnp.sum(before.astype(F32), axis=0, keepdims=True).astype(jnp.int32)
    rows = lax.broadcasted_iota(jnp.int32, (1, 256), 1)
    return owner * 32 + (rows >> 4) * 2 + rank


def own_slots(key, dp, states):
    mine = lax.broadcasted_iota(jnp.int32, (32, 256), 0) + dp * 32
    live = jnp.sum((mine == key).astype(F32), axis=1, keepdims=True)
    eye = lax.broadcasted_iota(jnp.int32, (32, 32), 0) == lax.broadcasted_iota(jnp.int32, (32, 32), 1)
    row_st = jnp.sum(jnp.where(eye, states, 0.0), axis=1, keepdims=True)
    return live, row_st, eye


def exchange(heads, inputs, owners_in, states_in, rb, sb,
             owners, states, hraw, iraw, ipf, hb, ib, hst, ibf, acc, gs, sown,
             ssh, rsh, ssi, rsi, ssy, rsy, ssc, rsc, sss, rss, ssg, rsg, loc):
    dp, a, z, shard, xl, y, c = place()
    other = 1 - a
    far_shard = (3 - xl) * 16 + y * 2 + c
    mate = xl * 16 + y * 2 + 1 - c
    fwd = lax.rem(y + 1 - 2 * c + 8, 8)
    back = lax.rem(y - 1 + 2 * c + 8, 8)
    fwd_shard = xl * 16 + fwd * 2 + c
    back_shard = xl * 16 + back * 2 + c
    right = (a * 8 + lax.rem(z + 1, 8), shard)
    left = (a * 8 + lax.rem(z + 7, 8), shard)

    def near(n):
        return a * 8 + lax.rem(z + n, 8)

    def far(n):
        return other * 8 + lax.rem(z + n, 8)

    peers = [near(n) for n in range(1, 8)] + [far(n) for n in range(8)]

    barrier = pltpu.get_barrier_semaphore()
    greeted = [(d, shard) for d in peers] + [(far(n), far_shard) for n in range(8)]
    greeted += [(dp, mate), (dp, fwd_shard), (dp, back_shard)]
    for who in greeted:
        pl.semaphore_signal(barrier, inc=1, device_id=who, device_id_type=MESH)

    local = [
        pltpu.make_async_copy(inputs.at[pl.ds(16 * y, 16)], iraw, loc.at[0]),
        pltpu.make_async_copy(heads, hraw, loc.at[1]),
        pltpu.make_async_copy(owners_in, owners, loc.at[4]),
        pltpu.make_async_copy(states_in, states, loc.at[5]),
    ]
    for cp in local:
        cp.start()

    local[1].wait()
    hb[dp] = hraw[...].astype(F32)
    local[0].wait()
    which = lax.broadcasted_iota(jnp.int32, (16, 2, 256), 1) == c

    def widen(d):
        at = pl.ds(pl.multiple_of(d * 256, 256), 256)
        ipf[d] = jnp.sum(jnp.where(which, iraw[:, :, at].astype(F32), 0.0), axis=1)

    pl.semaphore_wait(barrier, len(greeted))

    sent = []

    def send(src, dst, s_sem, r_sem, who):
        cp = pltpu.make_async_remote_copy(
            src_ref=src, dst_ref=dst, send_sem=s_sem, recv_sem=r_sem, device_id=who, device_id_type=MESH
        )
        cp.start()
        sent.append(cp)

    def arrived(ref, sem):
        pltpu.make_async_copy(ref, ref, sem).wait()

    count = [0]

    def piece(d, p):
        return hb.at[d, pl.ds(64 * p, 64)]

    def send_h(d, p, who):
        send(piece(d, p), piece(d, p), ssh.at[count[0]], rsh.at[d, p], who)
        count[0] += 1

    for p in range(2):
        send_h(dp, p, (far(0), shard))
    for i, n in enumerate((1, 7, 2, 6, 3, 5, 4)):
        d = near(n)
        widen(d)
        send(ipf.at[d], ib.at[c, y, dp], ssi.at[i], rsi.at[dp], (d, shard))
    for p in range(2):
        send_h(dp, p, right)
        send_h(dp, p, left)
    for i, n in enumerate((4, 3, 5, 2, 6, 1, 7, 0)):
        d = far(n)
        widen(d)
        send(ipf.at[d], ib.at[c, y, dp], ssi.at[7 + i], rsi.at[dp], (d, far_shard))

    widen(dp)
    ib[c, y, dp] = ipf[dp]

    local[2].wait()
    local[3].wait()
    key = row_keys(owners[...])
    k0 = lax.broadcasted_iota(jnp.int32, (16, 24, 1), 0) * 32 + lax.broadcasted_iota(jnp.int32, (16, 24, 1), 1)
    k1 = lax.broadcasted_iota(jnp.int32, (16, 8, 1), 0) * 32 + 24 + lax.broadcasted_iota(jnp.int32, (16, 8, 1), 1)
    pick0 = (k0.reshape(384, 1) == key).astype(F32).astype(BF16)
    pick1 = (k1.reshape(128, 1) == key).astype(F32).astype(BF16)
    live, row_st, _ = own_slots(key, dp, states[...])
    slot8 = lax.broadcasted_iota(jnp.int32, (32, 128), 0) >> 3
    lane = lax.broadcasted_iota(jnp.int32, (32, 128), 1)
    sown[...] = jnp.sum(jnp.where(slot8 == (lane >> 5), live * row_st, 0.0), axis=0, keepdims=True)
    for i, d in enumerate(peers):
        send(sown, sb.at[dp], sss.at[i], rss.at[dp], (d, shard))

    def got_h(d, p):
        arrived(piece(d, p), rsh.at[d, p])

    def pick_h(d):
        at = pl.ds(pl.multiple_of(d * 128, 128), 128)
        h = hb[d].astype(BF16)
        hst[0:384, at] = lax.dot_general(pick0, h, NT, preferred_element_type=F32).astype(BF16)
        hst[384:512, at] = lax.dot_general(pick1, h, NT, preferred_element_type=F32).astype(BF16)

    def narrow(core, yy, g):
        at = pl.ds(4 * quads[g], 4)
        ibf[core, at, yy] = ib[core, yy, at].astype(BF16)

    quads = (dp // 4, a * 2 + 1 - z // 4, other * 2 + z // 4, other * 2 + 1 - z // 4)

    def chunk(core, yy, g):
        return ib.at[core, yy, pl.ds(4 * quads[g], 4)]

    def send_y(yy, g, i, who):
        send(chunk(c, yy, g), chunk(c, yy, g), ssy.at[i, g], rsy.at[yy, g], (dp, who))

    def send_c(yy, g, i):
        send(chunk(c, yy, g), chunk(c, yy, g), ssc.at[i, g], rsc.at[yy, g], (dp, mate))

    def upstream(n):
        return lax.rem(y - n + 2 * n * c + 8, 8)

    def downstream(n):
        return lax.rem(y + n - 2 * n * c + 8, 8)

    def h_own(s):
        d, e = near(8 - s), near(s)
        for p in range(2):
            got_h(d, p)
            if s < 4:
                send_h(d, p, right)
                got_h(e, p)
                if s < 3:
                    send_h(e, p, left)
        pick_h(d)
        if s < 4:
            pick_h(e)

    def h_far(s):
        d, e = far(8 - s), far(s)
        for p in range(2):
            if 0 < s < 4:
                got_h(d, p)
                if s < 3:
                    send_h(d, p, right)
            got_h(e, p)
            if s == 0:
                send_h(e, p, right)
            if s < 4:
                send_h(e, p, left)
        if 0 < s < 4:
            pick_h(d)
        pick_h(e)

    def i_ring(s, *groups):
        for g in groups:
            if s == 0:
                for k in range(1 if g == 0 else 0, 4):
                    d = dp - z % 4 + lax.rem(z + k, 4) if g == 0 else 4 * quads[g] + k
                    arrived(ib.at[c, y, d], rsi.at[d])
                send_y(y, g, 0, fwd_shard)
                send_y(y, g, 1, back_shard)
                send_c(y, g, 0)
                narrow(c, y, g)
                continue
            up = upstream(s)
            arrived(chunk(c, up, g), rsy.at[up, g])
            if s < 4:
                send_y(up, g, 2 * s, fwd_shard)
            send_c(up, g, 2 * s - 1)
            if s < 4:
                down = downstream(s)
                arrived(chunk(c, down, g), rsy.at[down, g])
                if s < 3:
                    send_y(down, g, 2 * s + 1, back_shard)
                send_c(down, g, 2 * s)
                narrow(c, down, g)
            narrow(c, up, g)

    def tokens(g):
        for n in range(8):
            yy = lax.rem(y + n, 8)
            arrived(chunk(1 - c, yy, g), rsc.at[yy, g])
            narrow(1 - c, yy, g)
        at = pl.ds(pl.multiple_of(quads[g] * 512, 512), 512)
        w0 = ibf[0, pl.ds(4 * quads[g], 4)].reshape(512, 256)
        w1 = ibf[1, pl.ds(4 * quads[g], 4)].reshape(512, 256)
        g0 = jnp.dot(hst[0:384, at], w0, preferred_element_type=F32)
        g1 = jnp.dot(hst[384:512, at], w1, preferred_element_type=F32)
        if g == 0:
            acc[0:384, :] = g0
            acc[384:512, :] = g1
        else:
            acc[0:384, :] += g0
            acc[384:512, :] += g1

    pick_h(dp)
    h_own(1)
    i_ring(0, 0, 1)
    h_far(0)
    h_own(2)
    i_ring(0, 2, 3)
    i_ring(1, 0, 1)
    h_far(1)
    i_ring(1, 2, 3)
    h_own(3)
    i_ring(2, 0, 1)
    h_far(2)
    i_ring(2, 2, 3)
    h_own(4)
    i_ring(3, 0, 1)
    h_far(3)
    i_ring(3, 2, 3)
    i_ring(4, 0, 1)
    tokens(0)
    tokens(1)
    h_far(4)
    i_ring(4, 2, 3)
    tokens(2)
    tokens(3)

    for half in range(2):
        g0 = acc[0:384, half * 128:(half + 1) * 128].reshape(16, 24, 128)
        g1 = acc[384:512, half * 128:(half + 1) * 128].reshape(16, 8, 128)
        gs[:, half * 32:half * 32 + 24, :] = g0
        gs[:, half * 32 + 24:half * 32 + 32, :] = g1
        q0 = jnp.sum(jnp.sum((g0 * g0).reshape(16, 3, 8, 128), axis=0), axis=1)
        q1 = jnp.sum(jnp.sum(g1 * g1, axis=0), axis=0, keepdims=True)
        q = jnp.concatenate([q0, q1], axis=0)
        gs[:, 64 + half * 4:68 + half * 4, :] = jnp.broadcast_to(q[None], (16, 4, 128))

    for i, n in enumerate((4, 3, 5, 2, 6, 1, 7, 0)):
        d = far(n)
        send(gs.at[d], rb.at[dp], ssg.at[i], rsg.at[dp], (d, shard))
    for i, n in enumerate((4, 3, 5, 2, 6, 1, 7)):
        d = near(n)
        send(gs.at[d], rb.at[dp], ssg.at[8 + i], rsg.at[dp], (d, shard))
    keep = [
        pltpu.make_async_copy(gs.at[dp], rb.at[dp], loc.at[2]),
        pltpu.make_async_copy(sown, sb.at[dp], loc.at[3]),
    ]
    for cp in keep:
        cp.start()
    for d in peers:
        arrived(sb.at[d], rss.at[d])
    for d in peers:
        arrived(rb.at[d], rsg.at[d])
    for cp in keep:
        cp.wait()
    for cp in sent:
        cp.wait_send()


def finish(rb, sb, owners, states, params, cols, out_p, out_r, out_c):
    live, row_st, eye = own_slots(row_keys(owners[...]), lax.axis_index("dp"), states[...])
    slot8 = lax.broadcasted_iota(jnp.int32, (32, 128), 0) >> 3
    lane = lax.broadcasted_iota(jnp.int32, (32, 128), 1)
    sq = jnp.zeros((32, 128), F32)
    cs = jnp.zeros((4, 128), F32)
    for d in range(16):
        for half in range(2):
            g = rb[d, half * 32:half * 32 + 32, :]
            sq = sq + g * g
            cs = cs + rb[d, 64 + half * 4:68 + half * 4, :]
    row_val = 0.5 * row_st + 0.5 * (jnp.sum(sq, axis=1, keepdims=True) / 4096.0 + EPS_SQUARE)
    cs = cs + 64.0 * 32.0 * EPS_SQUARE
    all_cs = jnp.sum(jnp.broadcast_to(cs[:, None, :], (4, 8, 128)).reshape(32, 128), axis=1, keepdims=True)
    all_sb = jnp.sum(sb[...], axis=0)
    all_st = jnp.sum(jnp.where(lane == slot8 * 32, all_sb, 0.0), axis=1, keepdims=True)
    row_mean = (0.5 * all_st + 0.5 * (all_cs / 4096.0)) / 64.0
    by_row = 0.5 * lax.rsqrt(row_val / row_mean)
    out_r[...] = jnp.sum(jnp.where(eye, row_val * live, 0.0), axis=0, keepdims=True)
    for d in range(16):
        for half in range(2):
            at = d * 256 + half * 128
            q = rb[d, 64 + half * 4:68 + half * 4, :]
            new_col = 0.5 * cols[:, at:at + 128] + 0.5 * (q + 64.0 * EPS_SQUARE) / 64.0
            out_c[:, at:at + 128] = new_col
            by_col = jnp.broadcast_to(lax.rsqrt(new_col)[:, None, :], (4, 8, 128)).reshape(32, 128)
            g = rb[d, half * 32:half * 32 + 32, :]
            par = params[:, at:at + 128].astype(F32)
            out_p[:, at:at + 128] = ((par - g * by_row * by_col) * live).astype(BF16)


def on_device(head_terms, inputs, owner_list, param_slots, row_state, col_state):
    vm = pl.BlockSpec(memory_space=pltpu.VMEM)
    hbm = pl.BlockSpec(memory_space=pl.ANY)
    dma = pltpu.SemaphoreType.DMA
    owners = owner_list.reshape(1, 256)
    rb, sb = pl.pallas_call(
        exchange,
        out_shape=(jax.ShapeDtypeStruct((16, 72, 128), F32), jax.ShapeDtypeStruct((16, 1, 128), F32)),
        in_specs=[hbm] * 4,
        out_specs=(hbm, hbm),
        scratch_shapes=[
            pltpu.VMEM((1, 256), jnp.int32),
            pltpu.VMEM((1, 32), F32),
            pltpu.VMEM((128, 256), BF16),
            pltpu.VMEM((16, 2, 4096), BF16),
            pltpu.VMEM((16, 16, 256), F32),
            pltpu.VMEM((16, 128, 256), F32),
            pltpu.VMEM((2, 8, 16, 16, 256), F32),
            pltpu.VMEM((512, 2048), BF16),
            pltpu.VMEM((2, 16, 8, 16, 256), BF16),
            pltpu.VMEM((512, 256), F32),
            pltpu.VMEM((16, 72, 128), F32),
            pltpu.VMEM((1, 128), F32),
            dma((30,)), dma((16, 2)),
            dma((15,)), dma((16,)),
            dma((7, 4)), dma((8, 4)),
            dma((8, 4)), dma((8, 4)),
            dma((15,)), dma((16,)),
            dma((15,)), dma((16,)),
            dma((6,)),
        ],
        compiler_params=pltpu.CompilerParams(collective_id=0, has_side_effects=True),
    )(head_terms.reshape(128, 256), inputs, owners, row_state)
    new_params, new_rows, new_cols = pl.pallas_call(
        finish,
        out_shape=(
            jax.ShapeDtypeStruct((32, 4096), BF16),
            jax.ShapeDtypeStruct((1, 32), F32),
            jax.ShapeDtypeStruct((4, 4096), F32),
        ),
        in_specs=[vm] * 6,
        out_specs=(vm, vm, vm),
    )(rb, sb, owners, row_state, param_slots.reshape(32, 4096), col_state.reshape(4, 4096))
    return (new_params[None], new_rows, new_cols[None])


def solution(mesh):
    placed = (
        P("dp", "shard", None),
        P("dp", None, None),
        P("shard", None, None),
        P("shard", "dp", None),
        P("shard", "dp"),
        P("shard", None, None),
    )
    return jax.shard_map(
        on_device,
        mesh=mesh,
        in_specs=placed,
        out_specs=(P("shard", "dp", None), P("shard", "dp"), P("shard", None, None)),
        check_vma=False,
    )
```
